512 devices in a mesh: vec: 64 (over y, z), row: 8 (over x, core).
Axes of the slice: x: 4, y: 4, z: 16, core: 2. Of those that a mesh axis runs over, the one named last changes fastest.
Arguments:
- vectors: bfloat16 [8, 4096, 1024], P('row', 'vec'), may hold values from -6 to 6
- rotation: bfloat16 [1024, 1024], P(None, 'vec'), may hold values from -0.1875 to 0.1875
- blocks: bfloat16 [256, 8, 128, 128], P('row'), may hold values from -0.125 to 0.125
- column_blocks: int32 [256, 8], P('row'), may hold values from -2 to 257, as said below
Outputs:
- filtered: bfloat16 [8, 4096, 1024], P('row', 'vec')
The draws below stay inside these ranges and needn't reach their ends.
Inputs may be any that keep to these rules, and one draw needn't show every extreme that they name: `column_blocks`: block row r of partition p = r // 32 lists 8 distinct column blocks between p * 32 - 2 and p * 32 + 33; the first block row of every partition lists the lowest of these and the last one the highest; column blocks outside 0 to 255 stand for zeros.
All inputs are finite; a program needn't handle non-finite values.
Results may differ from the reference program's by a relative error of at most 0.006.
Values may be sent and summed in bfloat16 or wider, within the bound.
A program may use at most 64 MiB of HBM per device.

```python
import jax
import jax.numpy as jnp

K = 1024
BS = 128
NNZB = 8
HB = 2
STEPS = 4
RB = 32
NBLK = 256
ROWS_PART = 4096
NPART = 8


def draw_column_blocks(key, part):
    candidates = RB + 2 * HB
    subkeys = jax.random.split(key, NBLK)
    shuffled = jax.vmap(lambda sub: jax.random.permutation(sub, candidates))(subkeys)
    chosen = shuffled[:, :NNZB].astype(jnp.int32)
    within = jnp.arange(NBLK, dtype=jnp.int32) % RB
    required = jnp.where(within == 0, 0, jnp.where(within == RB - 1, candidates - 1, -1)).astype(jnp.int32)
    present = jnp.any(chosen == required[:, None], axis=1)
    replaced = jnp.where((required >= 0) & jnp.logical_not(present), required, chosen[:, NNZB - 1])
    chosen = chosen.at[:, NNZB - 1].set(replaced)
    first_block = jnp.arange(NBLK, dtype=jnp.int32) // RB * RB - HB
    return (chosen + first_block[:, None]).astype(jnp.int32)


def levels(own_key, shape, pieces, low, high):
    loudness = 1.0
    for position, shards_of in pieces:
        heights = jax.random.uniform(jax.random.fold_in(jax.random.fold_in(own_key, 6), position), (shards_of,), jnp.float32, low / len(pieces), high / len(pieces))
        loudness = loudness * jnp.repeat(jnp.exp(heights), shape[position] // shards_of).reshape((-1,) + (1,) * (len(shape) - 1 - position))
    return loudness


def bell_draw(rng, shape, spread, bound, cuts=(), kind=jnp.bfloat16):
    loudness = levels(rng, shape, cuts, -0.22, 0.18) if cuts else 1.0
    result = jax.random.normal(rng, shape, jnp.float32) * spread * loudness
    return jnp.minimum(jnp.maximum(result, -bound), bound).astype(kind)


def setup_inputs(seed: int = 0) -> dict:
    key_of = jax.random.split(jax.random.key(seed), 5)
    vectors = bell_draw(key_of[0], (NPART, ROWS_PART, K), 1.0, 6.0, ((0, 8), (1, 64)))
    rotation = bell_draw(key_of[1], (K, K), K ** -0.5, 0.1875, ((1, 64),))
    blocks = bell_draw(key_of[2], (NBLK, NNZB, BS, BS), (2 * NNZB * BS) ** -0.5, 0.125, ((0, 8),))
    column_blocks = draw_column_blocks(jax.random.fold_in(key_of[4], 71), 0)
    return dict(vectors=vectors, rotation=rotation, blocks=blocks, column_blocks=column_blocks)


centre = 0.3
half_width = 1.2


def apply_matrix(field, blocks, column_blocks):
    padded = jnp.pad(field, ((HB * BS, HB * BS), (0, 0)))
    stacked = padded.reshape(NBLK + 2 * HB, BS, K)
    picked = stacked[column_blocks + HB]
    product = jnp.einsum('rjab,rjbk->rak', blocks.astype(jnp.float32), picked.astype(jnp.float32))
    return product.reshape(NBLK * BS, K)


def reference(vectors, rotation, blocks, column_blocks):
    flattened = vectors.reshape(NBLK * BS, K)
    rotated = jnp.dot(flattened, rotation, preferred_element_type=jnp.float32).astype(jnp.bfloat16)
    previous = rotated.astype(jnp.float32)
    current = (apply_matrix(rotated, blocks, column_blocks) - centre * previous) / half_width
    for turn_index in range(STEPS - 1):
        operand = current.astype(jnp.bfloat16)
        following = 2.0 * (apply_matrix(operand, blocks, column_blocks) - centre * current) / half_width - previous
        previous = current
        current = following
    return current.astype(jnp.bfloat16).reshape(NPART, ROWS_PART, K)
```

```python
import functools

import jax
import jax.numpy as jnp
from jax import lax
from jax.experimental import pallas as pl
from jax.experimental.pallas import tpu as pltpu
from jax.sharding import PartitionSpec as P

MESH = pl.DeviceIdType.MESH
BS = 128
HB = 2
NNZB = 8
RB = 32
Z = 16
CORES = 2
F32 = jnp.float32
BF16 = jnp.bfloat16

centre = 0.3
half_width = 1.2


def take_all(ref, sem):
    pltpu.make_async_copy(ref, ref, sem).wait()


def halves(first, second):
    low = lax.broadcasted_iota(jnp.int32, first.shape, first.ndim - 1) < 64
    axis = first.ndim - 1
    return (
        jnp.where(low, first, pltpu.roll(second, 64, axis)),
        jnp.where(low, pltpu.roll(first, 64, axis), second),
    )


def kernel(
    nvec, nrow,
    v_hbm, rt_hbm, blk_hbm, col, out_ref,
    v_in, rt_in, blk, send1, recv1, u0, u1, u2, u3, fa, fb, send2, recv2, rall, fbuf,
    in_sem, s1, r1, s2, r2, hs, hr, gs, gr,
):
    me = lax.axis_index("vec")
    row = lax.axis_index("row")
    core = lax.rem(row, CORES)
    yy = me // Z
    xs = nrow // CORES
    ys = nvec // Z
    first = row * RB - HB

    v_copy = pltpu.make_async_copy(v_hbm, v_in, in_sem.at[0])
    r_copy = pltpu.make_async_copy(rt_hbm, rt_in, in_sem.at[1])
    b_copies = [
        pltpu.make_async_copy(blk_hbm.at[pl.ds(8 * q, 8)], blk.at[pl.ds(8 * q, 8)], in_sem.at[2 + q])
        for q in range(4)
    ]
    v_copy.start()
    r_copy.start()
    for c in b_copies:
        c.start()

    barrier = pltpu.get_barrier_semaphore()

    def greet(k, _):
        pl.semaphore_signal(barrier, inc=1, device_id={"vec": lax.rem(me + k, nvec)}, device_id_type=MESH)
        return 0

    lax.fori_loop(1, nvec, greet, 0)
    for k in range(1, nrow):
        pl.semaphore_signal(barrier, inc=1, device_id={"row": lax.rem(row + k, nrow)}, device_id_type=MESH)

    v_copy.wait()
    r_copy.wait()
    for t in range(4):
        pair = jnp.concatenate(
            [v_in[:, 256 * t : 256 * t + 128], v_in[:, 256 * t + 128 : 256 * t + 256]], axis=0
        )
        turned = pair.astype(F32).T.reshape(16, 8, 128).astype(BF16)
        send1[pl.ds(16 * t, 16)] = turned
    recv1[me] = send1[me]
    rall[row, me] = rt_in[:, pl.ds(pl.multiple_of(row * 128, 128), 128)]
    zero = jnp.zeros((HB, 16, 128), BF16)
    for u in (u0, u1, u2, u3):

        @pl.when(row == 0)
        def _():
            u[pl.ds(0, HB)] = zero

        @pl.when(row == nrow - 1)
        def _():
            u[pl.ds(RB + HB, HB)] = zero

    pl.semaphore_wait(barrier, nvec - 1 + nrow - 1)

    def deal(k, _):
        d = lax.rem(me + k, nvec)
        pltpu.make_async_remote_copy(
            send1.at[d], recv1.at[me], s1, r1, device_id={"vec": d}, device_id_type=MESH
        ).start()
        return 0

    lax.fori_loop(1, nvec, deal, 0)

    def along_z(k, _):
        d = yy * Z + lax.rem(me + k, Z)
        pltpu.make_async_remote_copy(
            rall.at[row, me], rall.at[row, me], gs.at[0], gr.at[0],
            device_id={"vec": d}, device_id_type=MESH,
        ).start()
        return 0

    lax.fori_loop(1, Z, along_z, 0)

    def halo(step, u):
        up = pltpu.make_async_remote_copy(
            u.at[pl.ds(RB, HB)], u.at[pl.ds(0, HB)], hs.at[step, 0], hr.at[step, 0],
            device_id={"row": jnp.minimum(row + 1, nrow - 1)}, device_id_type=MESH,
        )
        down = pltpu.make_async_remote_copy(
            u.at[pl.ds(HB, HB)], u.at[pl.ds(RB + HB, HB)], hs.at[step, 1], hr.at[step, 1],
            device_id={"row": jnp.maximum(row - 1, 0)}, device_id_type=MESH,
        )
        return up, down

    def halo_start(step, u):
        up, down = halo(step, u)
        pl.when(row < nrow - 1)(up.start)
        pl.when(row > 0)(down.start)

    def halo_wait(step, u):
        up, down = halo(step, u)
        pl.when(row > 0)(up.wait_recv)
        pl.when(row < nrow - 1)(down.wait_recv)

    def halo_sent(step, u):
        up, down = halo(step, u)
        pl.when(row < nrow - 1)(up.wait_send)
        pl.when(row > 0)(down.wait_send)

    take_all(recv1.at[pl.ds(0, nvec - 1)], r1)
    parts = recv1[...].astype(F32).reshape(RB, 2, 8, 128)
    low, high = halves(parts[:, 0], parts[:, 1])
    start = jnp.concatenate([low, high], axis=1)
    u0[pl.ds(HB, RB)] = start.astype(BF16)
    fa[...] = start
    halo_start(0, u0)

    take_all(rall.at[0, pl.ds(0, Z - 1)], gr.at[0])
    for k in range(1, ys):
        d = lax.rem(me + k * Z, nvec)
        pltpu.make_async_remote_copy(
            rall.at[row, pl.ds(yy * Z, Z)], rall.at[row, pl.ds(yy * Z, Z)], gs.at[1], gr.at[1],
            device_id={"vec": d}, device_id_type=MESH,
        ).start()

    for c in b_copies:
        c.wait()

    def product(u, r):
        left = jnp.concatenate([u[jnp.clip(col[j, r] - first, 0, RB + 2 * HB - 1)] for j in range(NNZB)], axis=1)
        right = jnp.concatenate([blk[r, j] for j in range(NNZB)], axis=1)
        return lax.dot_general(left, right, (((1,), (1,)), ((), ())), preferred_element_type=F32)

    def rows_of(turn, u, current, other, following, r):
        if turn == 0:
            made = (product(u, r) - centre * current[r]) / half_width
        else:
            made = 2.0 * (product(u, r) - centre * current[r]) / half_width - other[r]
        other[r] = made
        if following is not None:
            following[r + HB] = made.astype(BF16)
        return made

    def turn_of(turn, u, current, other, following):
        edge = functools.partial(rows_of, turn, u, current, other, following)
        for r in (0, 1, RB - 2, RB - 1):
            edge(r)
        halo_start(turn + 1, following)

        def inner(r, _):
            edge(r)
            return 0

        lax.fori_loop(HB, RB - HB, inner, 0, unroll=2)

    halo_wait(0, u0)
    turn_of(0, u0, fa, fb, u1)
    take_all(rall.at[0, pl.ds(0, nvec - Z)], gr.at[1])
    for k in range(1, xs):
        pltpu.make_async_remote_copy(
            rall.at[row], rall.at[row], gs.at[2], gr.at[2],
            device_id={"row": lax.rem(row + k * CORES, nrow)}, device_id_type=MESH,
        ).start()
    mate = row + 1 - 2 * core
    pltpu.make_async_remote_copy(
        rall.at[row], rall.at[row], gs.at[3], gr.at[3], device_id={"row": mate}, device_id_type=MESH
    ).start()
    halo_wait(1, u1)
    turn_of(1, u1, fb, fa, u2)
    halo_wait(2, u2)
    turn_of(2, u2, fa, fb, u3)
    halo_wait(3, u3)

    def last(k, _):
        r = lax.rem(me // 2 + k, RB)
        made = rows_of(3, u3, fb, fa, None, r)
        even, odd = halves(made[:8], made[8:])
        send2[2 * r] = even.astype(BF16)
        send2[2 * r + 1] = odd.astype(BF16)
        for side in range(2):
            d = 2 * r + side

            @pl.when(d != me)
            def _():
                pltpu.make_async_remote_copy(
                    send2.at[d], recv2.at[me], s2, r2, device_id={"vec": d}, device_id_type=MESH
                ).start()

        return 0

    lax.fori_loop(0, RB, last, 0)
    recv2[me] = send2[me]

    take_all(rall.at[pl.ds(0, xs - 1)], gr.at[2])
    for k in range(1, xs):
        other = lax.rem(row + k * CORES, nrow)
        pltpu.make_async_remote_copy(
            rall.at[other], rall.at[other], gs.at[4], gr.at[4], device_id={"row": mate}, device_id_type=MESH
        ).start()

    take_all(recv2.at[pl.ds(0, nvec - 1)], r2)
    for t in range(4):
        turned = recv2[pl.ds(16 * t, 16)].astype(F32).reshape(128, 128).T.astype(BF16)
        fbuf[:, 256 * t : 256 * t + 128] = turned[:64]
        fbuf[:, 256 * t + 128 : 256 * t + 256] = turned[64:]

    take_all(rall.at[0], gr.at[3])
    take_all(rall.at[pl.ds(0, xs - 1)], gr.at[4])
    total = jnp.zeros((64, 1024), F32)
    for t in range(4):
        right = jnp.concatenate(
            [rall[2 * t].reshape(1024, 128), rall[2 * t + 1].reshape(1024, 128)], axis=1
        )
        total += lax.dot_general(
            fbuf[:, 256 * t : 256 * t + 256], right, (((1,), (1,)), ((), ())), preferred_element_type=F32
        )
    out_ref[...] = total.astype(BF16)

    take_all(send1.at[pl.ds(0, nvec - 1)], s1)
    take_all(send2.at[pl.ds(0, nvec - 1)], s2)
    for step, u in enumerate((u0, u1, u2, u3)):
        halo_sent(step, u)
    take_all(rall.at[0, pl.ds(0, Z - 1)], gs.at[0])
    take_all(rall.at[0, pl.ds(0, nvec - Z)], gs.at[1])
    take_all(rall.at[pl.ds(0, xs - 1)], gs.at[2])
    take_all(rall.at[0], gs.at[3])
    take_all(rall.at[pl.ds(0, xs - 1)], gs.at[4])


def local(nvec, nrow, vectors, rotation, blocks, column_blocks):
    whole = pl.BlockSpec(memory_space=pltpu.HBM)
    out = pl.pallas_call(
        functools.partial(kernel, nvec, nrow),
        out_shape=jax.ShapeDtypeStruct((64, 1024), BF16),
        in_specs=[whole, whole, whole, pl.BlockSpec(memory_space=pltpu.SMEM)],
        out_specs=pl.BlockSpec(memory_space=pltpu.VMEM),
        scratch_shapes=[
            pltpu.VMEM((64, 1024), BF16),
            pltpu.VMEM((16, 1024), BF16),
            pltpu.VMEM((RB, NNZB, BS, BS), BF16),
            pltpu.VMEM((nvec, 8, 128), BF16),
            pltpu.VMEM((nvec, 8, 128), BF16),
            pltpu.VMEM((RB + 2 * HB, 16, BS), BF16),
            pltpu.VMEM((RB + 2 * HB, 16, BS), BF16),
            pltpu.VMEM((RB + 2 * HB, 16, BS), BF16),
            pltpu.VMEM((RB + 2 * HB, 16, BS), BF16),
            pltpu.VMEM((RB, 16, BS), F32),
            pltpu.VMEM((RB, 16, BS), F32),
            pltpu.VMEM((nvec, 8, 128), BF16),
            pltpu.VMEM((nvec, 8, 128), BF16),
            pltpu.VMEM((nrow, nvec, 16, 128), BF16),
            pltpu.VMEM((64, 1024), BF16),
            pltpu.SemaphoreType.DMA((6,)),
            pltpu.SemaphoreType.DMA,
            pltpu.SemaphoreType.DMA,
            pltpu.SemaphoreType.DMA,
            pltpu.SemaphoreType.DMA,
            pltpu.SemaphoreType.DMA((4, 2)),
            pltpu.SemaphoreType.DMA((4, 2)),
            pltpu.SemaphoreType.DMA((5,)),
            pltpu.SemaphoreType.DMA((5,)),
        ],
        compiler_params=pltpu.CompilerParams(
            collective_id=0, has_side_effects=True, vmem_limit_bytes=60 << 20
        ),
    )(vectors[0], rotation.T, blocks, column_blocks.T)
    return out[None]


def solution(mesh):
    placed = (P("row", "vec", None), P(None, "vec"), P("row", None, None, None), P("row", None))
    return jax.shard_map(
        functools.partial(local, mesh.shape["vec"], mesh.shape["row"]),
        mesh=mesh, in_specs=placed, out_specs=P("row", "vec", None), check_vma=False,
    )
```

```python
import functools

import jax
import jax.numpy as jnp
from jax import lax
from jax.experimental import pallas as pl
from jax.experimental.pallas import tpu as pltpu
from jax.sharding import PartitionSpec as P

MESH = pl.DeviceIdType.MESH
BS = 128
HB = 2
NNZB = 8
RB = 32
Z = 16
CORES = 2
F32 = jnp.float32
BF16 = jnp.bfloat16

centre = 0.3
half_width = 1.2


def take_all(ref, sem):
    pltpu.make_async_copy(ref, ref, sem).wait()


def both_ways(q, at, size):
    return lax.rem(at + (2 * lax.rem(q, 2) - 1) * ((q + 1) // 2) + size, size)


def halves(first, second):
    low = lax.broadcasted_iota(jnp.int32, first.shape, first.ndim - 1) < 64
    axis = first.ndim - 1
    return (
        jnp.where(low, first, pltpu.roll(second, 64, axis)),
        jnp.where(low, pltpu.roll(first, 64, axis), second),
    )


def kernel(
    nvec, nrow,
    v_hbm, rt_hbm, blk_hbm, col_hbm, out_ref,
    col, v_in, rt_in, blk, send1, recv1, u0, u1, u2, u3, fa, fb, send2, recv2, rall, fbuf,
    in_sem, s1, r1, s2, r2, hs, hr, gs, gr,
):
    me = lax.axis_index("vec")
    row = lax.axis_index("row")
    core = lax.rem(row, CORES)
    yy = me // Z
    zz = lax.rem(me, Z)
    xs = nrow // CORES
    ys = nvec // Z
    first = row * RB - HB

    v_copy = pltpu.make_async_copy(v_hbm, v_in, in_sem.at[0])
    r_copy = pltpu.make_async_copy(rt_hbm, rt_in, in_sem.at[1])
    b_copies = [
        pltpu.make_async_copy(blk_hbm.at[pl.ds(8 * q, 8)], blk.at[pl.ds(8 * q, 8)], in_sem.at[2 + q])
        for q in range(4)
    ]
    c_copy = pltpu.make_async_copy(col_hbm, col, in_sem.at[6])
    v_copy.start()
    r_copy.start()
    c_copy.start()
    for c in b_copies:
        c.start()

    barrier = pltpu.get_barrier_semaphore()

    lines = [lax.rem(yy + dy, ys) * Z for dy in (2, 3, 1, 0)]

    def farthest_first(visit):
        def layer(k, _):
            z = both_ways(Z - 1 - k, zz, Z)
            for line in lines:
                visit(line + z)
            return 0

        lax.fori_loop(0, Z - 1, layer, 0)
        for line in lines[:-1]:
            visit(line + zz)

    def greet(d):
        pl.semaphore_signal(barrier, inc=1, device_id={"vec": d}, device_id_type=MESH)

    farthest_first(greet)
    for k in range(1, nrow):
        pl.semaphore_signal(barrier, inc=1, device_id={"row": lax.rem(row + k, nrow)}, device_id_type=MESH)

    v_copy.wait()
    r_copy.wait()
    for t in range(4):
        pair = jnp.concatenate(
            [v_in[:, 256 * t : 256 * t + 128], v_in[:, 256 * t + 128 : 256 * t + 256]], axis=0
        )
        turned = pair.astype(F32).T.reshape(16, 8, 128).astype(BF16)
        send1[pl.ds(16 * t, 16)] = turned
    recv1[me] = send1[me]
    rall[row, me] = rt_in[:, pl.ds(pl.multiple_of(row * 128, 128), 128)]
    zero = jnp.zeros((HB, 16, 128), BF16)
    for u in (u0, u1, u2, u3):

        @pl.when(row == 0)
        def _():
            u[pl.ds(0, HB)] = zero

        @pl.when(row == nrow - 1)
        def _():
            u[pl.ds(RB + HB, HB)] = zero

    pl.semaphore_wait(barrier, nvec - 1 + nrow - 1)

    def deal(d):
        pltpu.make_async_remote_copy(
            send1.at[d], recv1.at[me], s1, r1, device_id={"vec": d}, device_id_type=MESH
        ).start()

    farthest_first(deal)

    def along_z(k, _):
        d = yy * Z + both_ways(Z - k, zz, Z)
        pltpu.make_async_remote_copy(
            rall.at[row, me], rall.at[row, me], gs.at[0], gr.at[0],
            device_id={"vec": d}, device_id_type=MESH,
        ).start()
        return 0

    lax.fori_loop(1, Z, along_z, 0)

    def halo(step, u):
        up = pltpu.make_async_remote_copy(
            u.at[pl.ds(RB, HB)], u.at[pl.ds(0, HB)], hs.at[step, 0], hr.at[step, 0],
            device_id={"row": jnp.minimum(row + 1, nrow - 1)}, device_id_type=MESH,
        )
        down = pltpu.make_async_remote_copy(
            u.at[pl.ds(HB, HB)], u.at[pl.ds(RB + HB, HB)], hs.at[step, 1], hr.at[step, 1],
            device_id={"row": jnp.maximum(row - 1, 0)}, device_id_type=MESH,
        )
        return up, down

    def halo_start(step, u):
        up, down = halo(step, u)
        pl.when(row < nrow - 1)(up.start)
        pl.when(row > 0)(down.start)

    def halo_wait(step, u):
        up, down = halo(step, u)
        pl.when(row > 0)(up.wait_recv)
        pl.when(row < nrow - 1)(down.wait_recv)

    def halo_sent(step, u):
        up, down = halo(step, u)
        pl.when(row < nrow - 1)(up.wait_send)
        pl.when(row > 0)(down.wait_send)

    for c in b_copies:
        c.wait()

    def flip(r, _):
        for j in range(NNZB):
            blk[r, j] = blk[r, j].T
        return 0

    lax.fori_loop(0, RB, flip, 0)
    c_copy.wait()
    take_all(recv1.at[pl.ds(0, nvec - 1)], r1)
    parts = recv1[...].astype(F32).reshape(RB, 2, 8, 128)
    low, high = halves(parts[:, 0], parts[:, 1])
    start = jnp.concatenate([low, high], axis=1)
    u0[pl.ds(HB, RB)] = start.astype(BF16)
    fa[...] = start
    halo_start(0, u0)

    def product(u, r):
        left = jnp.concatenate([u[jnp.clip(col[j, r] - first, 0, RB + 2 * HB - 1)] for j in range(NNZB)], axis=1)
        right = jnp.concatenate([blk[r, j] for j in range(NNZB)], axis=0)
        return jnp.dot(left, right, preferred_element_type=F32)

    def rows_of(turn, u, current, other, following, r):
        if turn == 0:
            made = (product(u, r) - centre * current[r]) / half_width
        else:
            made = 2.0 * (product(u, r) - centre * current[r]) / half_width - other[r]
        other[r] = made
        if following is not None:
            following[r + HB] = made.astype(BF16)
        return made

    def turn_of(turn, u, current, other, following):
        edge = functools.partial(rows_of, turn, u, current, other, following)
        for r in (0, 1, RB - 2, RB - 1):
            edge(r)
        halo_start(turn + 1, following)

        def inner(r, _):
            edge(r)
            return 0

        spread(turn)
        lax.fori_loop(HB, RB - HB, inner, 0, unroll=14)

    mate = row + 1 - 2 * core
    right = lax.rem(row + CORES, nrow)
    left = lax.rem(row + nrow - CORES, nrow)
    opposite = lax.rem(row + 2 * CORES, nrow)
    half = nvec // 2

    def pass_on(n, held, part, target):
        piece = rall.at[held, pl.ds(part * half, half)]
        return pltpu.make_async_remote_copy(
            piece, piece, gs.at[n], gr.at[n], device_id={"row": target}, device_id_type=MESH
        )

    def to_mate(n, held):
        return pltpu.make_async_remote_copy(
            rall.at[held], rall.at[held], gs.at[n], gr.at[n], device_id={"row": mate}, device_id_type=MESH
        )

    def spread(turn):
        if turn == 1:
            take_all(rall.at[0, pl.ds(0, nvec - Z)], gr.at[1])
            pass_on(2, row, 0, right).start()
            pass_on(3, row, 1, left).start()
            to_mate(8, row).start()
        if turn == 2:
            pass_on(4, row, 1, right).start()
            pass_on(5, row, 0, left).start()
        if turn == 3:
            pass_on(2, left, 0, right).wait_recv()
            pass_on(3, right, 1, left).wait_recv()
            pass_on(6, left, 0, right).start()
            pass_on(7, right, 1, left).start()

    take_all(rall.at[0, pl.ds(0, Z - 1)], gr.at[0])
    for k in range(1, ys):
        d = lax.rem(me + k * Z, nvec)
        pltpu.make_async_remote_copy(
            rall.at[row, pl.ds(yy * Z, Z)], rall.at[row, pl.ds(yy * Z, Z)], gs.at[1], gr.at[1],
            device_id={"vec": d}, device_id_type=MESH,
        ).start()

    halo_wait(0, u0)
    turn_of(0, u0, fa, fb, u1)
    halo_wait(1, u1)
    turn_of(1, u1, fb, fa, u2)
    halo_wait(2, u2)
    turn_of(2, u2, fa, fb, u3)
    halo_wait(3, u3)
    zpairs = Z // 2

    def finish(r):
        made = rows_of(3, u3, fb, fa, None, r)
        even, odd = halves(made[:8], made[8:])
        send2[2 * r] = even.astype(BF16)
        send2[2 * r + 1] = odd.astype(BF16)

    def give(d):
        @pl.when(d != me)
        def _():
            pltpu.make_async_remote_copy(
                send2.at[d], recv2.at[me], s2, r2, device_id={"vec": d}, device_id_type=MESH
            ).start()

    def last(g, _):
        group = [
            lax.rem(yy + dy, ys) * zpairs + (g + far)
            for dy in range(ys)
            for far in (0, zpairs // 2)
        ]
        for r in group:
            finish(r)
        for r in group:
            give(2 * r)
            give(2 * r + 1)
        return 0

    lax.fori_loop(0, zpairs // 2, last, 0)
    recv2[me] = send2[me]
    spread(3)
    pass_on(4, left, 1, right).wait_recv()
    pass_on(5, right, 0, left).wait_recv()
    to_mate(9, left).start()
    to_mate(10, right).start()
    pass_on(6, opposite, 0, right).wait_recv()
    pass_on(7, opposite, 1, left).wait_recv()
    to_mate(11, opposite).start()

    take_all(recv2.at[pl.ds(0, nvec - 1)], r2)
    for t in range(4):
        turned = recv2[pl.ds(16 * t, 16)].astype(F32).reshape(128, 128).T.astype(BF16)
        fbuf[:, 256 * t : 256 * t + 128] = turned[:64]
        fbuf[:, 256 * t + 128 : 256 * t + 256] = turned[64:]

    for n in range(8, 12):
        take_all(rall.at[0], gr.at[n])
    total = jnp.zeros((64, 1024), F32)
    for t in range(4):
        right = jnp.concatenate(
            [rall[2 * t].reshape(1024, 128), rall[2 * t + 1].reshape(1024, 128)], axis=1
        )
        total += lax.dot_general(
            fbuf[:, 256 * t : 256 * t + 256], right, (((1,), (1,)), ((), ())), preferred_element_type=F32
        )
    out_ref[...] = total.astype(BF16)

    take_all(send1.at[pl.ds(0, nvec - 1)], s1)
    take_all(send2.at[pl.ds(0, nvec - 1)], s2)
    for step, u in enumerate((u0, u1, u2, u3)):
        halo_sent(step, u)
    take_all(rall.at[0, pl.ds(0, Z - 1)], gs.at[0])
    take_all(rall.at[0, pl.ds(0, nvec - Z)], gs.at[1])
    for n in range(2, 8):
        take_all(rall.at[0, pl.ds(0, half)], gs.at[n])
    for n in range(8, 12):
        take_all(rall.at[0], gs.at[n])


def local(nvec, nrow, vectors, rotation, blocks, column_blocks):
    whole = pl.BlockSpec(memory_space=pltpu.HBM)
    out = pl.pallas_call(
        functools.partial(kernel, nvec, nrow),
        out_shape=jax.ShapeDtypeStruct((64, 1024), BF16),
        in_specs=[whole] * 4,
        out_specs=pl.BlockSpec(memory_space=pltpu.VMEM),
        scratch_shapes=[
            pltpu.SMEM((NNZB, RB), jnp.int32),
            pltpu.VMEM((64, 1024), BF16),
            pltpu.VMEM((16, 1024), BF16),
            pltpu.VMEM((RB, NNZB, BS, BS), BF16),
            pltpu.VMEM((nvec, 8, 128), BF16),
            pltpu.VMEM((nvec, 8, 128), BF16),
            pltpu.VMEM((RB + 2 * HB, 16, BS), BF16),
            pltpu.VMEM((RB + 2 * HB, 16, BS), BF16),
            pltpu.VMEM((RB + 2 * HB, 16, BS), BF16),
            pltpu.VMEM((RB + 2 * HB, 16, BS), BF16),
            pltpu.VMEM((RB, 16, BS), F32),
            pltpu.VMEM((RB, 16, BS), F32),
            pltpu.VMEM((nvec, 8, 128), BF16),
            pltpu.VMEM((nvec, 8, 128), BF16),
            pltpu.VMEM((nrow, nvec, 16, 128), BF16),
            pltpu.VMEM((64, 1024), BF16),
            pltpu.SemaphoreType.DMA((7,)),
            pltpu.SemaphoreType.DMA,
            pltpu.SemaphoreType.DMA,
            pltpu.SemaphoreType.DMA,
            pltpu.SemaphoreType.DMA,
            pltpu.SemaphoreType.DMA((4, 2)),
            pltpu.SemaphoreType.DMA((4, 2)),
            pltpu.SemaphoreType.DMA((12,)),
            pltpu.SemaphoreType.DMA((12,)),
        ],
        compiler_params=pltpu.CompilerParams(
            collective_id=0, has_side_effects=True, vmem_limit_bytes=60 << 20
        ),
    )(vectors[0], rotation.T, blocks, column_blocks.T)
    return out[None]


def solution(mesh):
    placed = (P("row", "vec", None), P(None, "vec"), P("row", None, None, None), P("row", None))
    return jax.shard_map(
        functools.partial(local, mesh.shape["vec"], mesh.shape["row"]),
        mesh=mesh, in_specs=placed, out_specs=P("row", "vec", None), check_vma=False,
    )
```

```python
import functools

import jax
import jax.numpy as jnp
from jax import lax
from jax.experimental import pallas as pl
from jax.experimental.pallas import tpu as pltpu
from jax.sharding import PartitionSpec as P

MESH = pl.DeviceIdType.MESH
BS = 128
HB = 2
NNZB = 8
RB = 32
Z = 16
CORES = 2
F32 = jnp.float32
BF16 = jnp.bfloat16

centre = 0.3
half_width = 1.2


def take_all(ref, sem):
    pltpu.make_async_copy(ref, ref, sem).wait()


def both_ways(q, at, size):
    return lax.rem(at + (2 * lax.rem(q, 2) - 1) * ((q + 1) // 2) + size, size)


def halves(first, second):
    low = lax.broadcasted_iota(jnp.int32, first.shape, first.ndim - 1) < 64
    axis = first.ndim - 1
    return (
        jnp.where(low, first, pltpu.roll(second, 64, axis)),
        jnp.where(low, pltpu.roll(first, 64, axis), second),
    )


def kernel(
    nvec, nrow,
    v_hbm, rt_hbm, blk_hbm, col_hbm, out_ref,
    col, v_in, rt_in, blk, send1, recv1, u0, u1, u2, u3, fa, fb, send2, recv2, rall, fbuf,
    in_sem, s1, r1, s2, r2, hs, hr, gs, gr,
):
    me = lax.axis_index("vec")
    row = lax.axis_index("row")
    core = lax.rem(row, CORES)
    yy = me // Z
    zz = lax.rem(me, Z)
    xs = nrow // CORES
    ys = nvec // Z
    first = row * RB - HB

    v_copy = pltpu.make_async_copy(v_hbm, v_in, in_sem.at[0])
    r_copy = pltpu.make_async_copy(rt_hbm, rt_in, in_sem.at[1])
    b_copies = [
        pltpu.make_async_copy(blk_hbm.at[pl.ds(8 * q, 8)], blk.at[pl.ds(8 * q, 8)], in_sem.at[2 + q])
        for q in range(4)
    ]
    c_copy = pltpu.make_async_copy(col_hbm, col, in_sem.at[6])
    v_copy.start()
    r_copy.start()
    c_copy.start()
    for c in b_copies:
        c.start()

    barrier = pltpu.get_barrier_semaphore()

    lines = [lax.rem(yy + dy, ys) * Z for dy in (2, 3, 1, 0)]

    def farthest_first(visit):
        def layer(k, _):
            z = both_ways(Z - 1 - k, zz, Z)
            for line in lines:
                visit(line + z)
            return 0

        lax.fori_loop(0, Z - 1, layer, 0)
        for line in lines[:-1]:
            visit(line + zz)

    def greet(d):
        pl.semaphore_signal(barrier, inc=1, device_id={"vec": d}, device_id_type=MESH)

    farthest_first(greet)
    for k in range(1, nrow):
        pl.semaphore_signal(barrier, inc=1, device_id={"row": lax.rem(row + k, nrow)}, device_id_type=MESH)

    v_copy.wait()
    r_copy.wait()
    for t in range(4):
        pair = jnp.concatenate(
            [v_in[:, 256 * t : 256 * t + 128], v_in[:, 256 * t + 128 : 256 * t + 256]], axis=0
        )
        turned = pair.astype(F32).T.reshape(16, 8, 128).astype(BF16)
        send1[pl.ds(16 * t, 16)] = turned
    recv1[me] = send1[me]
    rall[row, me] = rt_in[:, pl.ds(pl.multiple_of(row * 128, 128), 128)]
    zero = jnp.zeros((HB, 16, 128), BF16)
    for u in (u0, u1, u2, u3):

        @pl.when(row == 0)
        def _():
            u[pl.ds(0, HB)] = zero

        @pl.when(row == nrow - 1)
        def _():
            u[pl.ds(RB + HB, HB)] = zero

    pl.semaphore_wait(barrier, nvec - 1 + nrow - 1)

    def deal(d):
        pltpu.make_async_remote_copy(
            send1.at[d], recv1.at[me], s1, r1, device_id={"vec": d}, device_id_type=MESH
        ).start()

    farthest_first(deal)

    def along_z(k, _):
        d = yy * Z + both_ways(Z - k, zz, Z)
        pltpu.make_async_remote_copy(
            rall.at[row, me], rall.at[row, me], gs.at[0], gr.at[0],
            device_id={"vec": d}, device_id_type=MESH,
        ).start()
        return 0

    lax.fori_loop(1, Z, along_z, 0)

    def halo(step, u):
        up = pltpu.make_async_remote_copy(
            u.at[pl.ds(RB, HB)], u.at[pl.ds(0, HB)], hs.at[step, 0], hr.at[step, 0],
            device_id={"row": jnp.minimum(row + 1, nrow - 1)}, device_id_type=MESH,
        )
        down = pltpu.make_async_remote_copy(
            u.at[pl.ds(HB, HB)], u.at[pl.ds(RB + HB, HB)], hs.at[step, 1], hr.at[step, 1],
            device_id={"row": jnp.maximum(row - 1, 0)}, device_id_type=MESH,
        )
        return up, down

    def halo_start(step, u):
        up, down = halo(step, u)
        pl.when(row < nrow - 1)(up.start)
        pl.when(row > 0)(down.start)

    def halo_wait(step, u):
        up, down = halo(step, u)
        pl.when(row > 0)(up.wait_recv)
        pl.when(row < nrow - 1)(down.wait_recv)

    def halo_sent(step, u):
        up, down = halo(step, u)
        pl.when(row < nrow - 1)(up.wait_send)
        pl.when(row > 0)(down.wait_send)

    for c in b_copies:
        c.wait()

    def flip(r, _):
        for j in range(NNZB):
            blk[r, j] = blk[r, j].T
        return 0

    lax.fori_loop(0, RB, flip, 0)
    c_copy.wait()
    take_all(recv1.at[pl.ds(0, nvec - 1)], r1)
    parts = recv1[...].astype(F32).reshape(RB, 2, 8, 128)
    low, high = halves(parts[:, 0], parts[:, 1])
    start = jnp.concatenate([low, high], axis=1)
    u0[pl.ds(HB, RB)] = start.astype(BF16)
    fa[...] = start
    halo_start(0, u0)

    def product(u, r):
        left = jnp.concatenate([u[jnp.clip(col[j, r] - first, 0, RB + 2 * HB - 1)] for j in range(NNZB)], axis=1)
        right = jnp.concatenate([blk[r, j] for j in range(NNZB)], axis=0)
        return jnp.dot(left, right, preferred_element_type=F32)

    def rows_of(turn, u, current, other, following, r):
        if turn == 0:
            made = (product(u, r) - centre * current[r]) / half_width
        else:
            made = 2.0 * (product(u, r) - centre * current[r]) / half_width - other[r]
        other[r] = made
        if following is not None:
            following[r + HB] = made.astype(BF16)
        return made

    def turn_of(turn, u, current, other, following):
        edge = functools.partial(rows_of, turn, u, current, other, following)
        for r in (0, 1, RB - 2, RB - 1):
            edge(r)
        halo_start(turn + 1, following)

        def inner(r, _):
            edge(r)
            return 0

        spread(turn)
        lax.fori_loop(HB, RB - HB, inner, 0, unroll=14)

    mate = row + 1 - 2 * core
    right = lax.rem(row + CORES, nrow)
    left = lax.rem(row + nrow - CORES, nrow)
    opposite = lax.rem(row + 2 * CORES, nrow)
    half = nvec // 2

    def pass_on(n, held, part, target):
        piece = rall.at[held, pl.ds(part * half, half)]
        return pltpu.make_async_remote_copy(
            piece, piece, gs.at[n], gr.at[n], device_id={"row": target}, device_id_type=MESH
        )

    def to_mate(n, held):
        return pltpu.make_async_remote_copy(
            rall.at[held], rall.at[held], gs.at[n], gr.at[n], device_id={"row": mate}, device_id_type=MESH
        )

    def spread(turn):
        if turn == 1:
            take_all(rall.at[0, pl.ds(0, nvec - Z)], gr.at[1])
            pass_on(2, row, 0, right).start()
            pass_on(3, row, 1, left).start()
            to_mate(8, row).start()
        if turn == 2:
            pass_on(4, row, 1, right).start()
            pass_on(5, row, 0, left).start()
        if turn == 3:
            pass_on(2, left, 0, right).wait_recv()
            pass_on(3, right, 1, left).wait_recv()
            pass_on(6, left, 0, right).start()
            pass_on(7, right, 1, left).start()

    take_all(rall.at[0, pl.ds(0, Z - 1)], gr.at[0])
    for k in range(1, ys):
        d = lax.rem(me + k * Z, nvec)
        pltpu.make_async_remote_copy(
            rall.at[row, pl.ds(yy * Z, Z)], rall.at[row, pl.ds(yy * Z, Z)], gs.at[1], gr.at[1],
            device_id={"vec": d}, device_id_type=MESH,
        ).start()

    halo_wait(0, u0)
    turn_of(0, u0, fa, fb, u1)
    halo_wait(1, u1)
    turn_of(1, u1, fb, fa, u2)
    halo_wait(2, u2)
    turn_of(2, u2, fa, fb, u3)
    halo_wait(3, u3)
    zpairs = Z // 2

    def finish(r):
        made = rows_of(3, u3, fb, fa, None, r)
        even, odd = halves(made[:8], made[8:])
        send2[2 * r] = even.astype(BF16)
        send2[2 * r + 1] = odd.astype(BF16)

    def give(d):
        @pl.when(d != me)
        def _():
            pltpu.make_async_remote_copy(
                send2.at[d], recv2.at[me], s2, r2, device_id={"vec": d}, device_id_type=MESH
            ).start()

    def last(g, _):
        group = [
            lax.rem(yy + dy, ys) * zpairs + (g + far)
            for dy in range(ys)
            for far in (0, zpairs // 2)
        ]
        for r in group:
            finish(r)
        for r in group:
            give(2 * r)
            give(2 * r + 1)
        return 0

    lax.fori_loop(0, zpairs // 2, last, 0)
    recv2[me] = send2[me]
    spread(3)
    pass_on(4, left, 1, right).wait_recv()
    pass_on(5, right, 0, left).wait_recv()
    to_mate(9, left).start()
    to_mate(10, right).start()
    pass_on(6, opposite, 0, right).wait_recv()
    pass_on(7, opposite, 1, left).wait_recv()
    to_mate(11, opposite).start()

    take_all(recv2.at[pl.ds(0, nvec - 1)], r2)
    for t in range(4):
        turned = recv2[pl.ds(16 * t, 16)].astype(F32).reshape(128, 128).T.astype(BF16)
        fbuf[:, 256 * t : 256 * t + 128] = turned[:64]
        fbuf[:, 256 * t + 128 : 256 * t + 256] = turned[64:]

    for n in range(8, 12):
        take_all(rall.at[0], gr.at[n])
    total = jnp.zeros((64, 1024), F32)
    for t in range(4):
        right = jnp.concatenate(
            [rall[2 * t].reshape(1024, 128), rall[2 * t + 1].reshape(1024, 128)], axis=1
        )
        total += lax.dot_general(
            fbuf[:, 256 * t : 256 * t + 256], right, (((1,), (1,)), ((), ())), preferred_element_type=F32
        )
    out_ref[...] = total.astype(BF16)

    take_all(send1.at[pl.ds(0, nvec - 1)], s1)
    take_all(send2.at[pl.ds(0, nvec - 1)], s2)
    for step, u in enumerate((u0, u1, u2, u3)):
        halo_sent(step, u)
    take_all(rall.at[0, pl.ds(0, Z - 1)], gs.at[0])
    take_all(rall.at[0, pl.ds(0, nvec - Z)], gs.at[1])
    for n in range(2, 8):
        take_all(rall.at[0, pl.ds(0, half)], gs.at[n])
    for n in range(8, 12):
        take_all(rall.at[0], gs.at[n])


def local(nvec, nrow, vectors, rotation, blocks, column_blocks):
    whole = pl.BlockSpec(memory_space=pltpu.HBM)
    out = pl.pallas_call(
        functools.partial(kernel, nvec, nrow),
        out_shape=jax.ShapeDtypeStruct((64, 1024), BF16),
        in_specs=[whole] * 4,
        out_specs=pl.BlockSpec(memory_space=pltpu.VMEM),
        scratch_shapes=[
            pltpu.SMEM((NNZB, RB), jnp.int32),
            pltpu.VMEM((64, 1024), BF16),
            pltpu.VMEM((16, 1024), BF16),
            pltpu.VMEM((RB, NNZB, BS, BS), BF16),
            pltpu.VMEM((nvec, 8, 128), BF16),
            pltpu.VMEM((nvec, 8, 128), BF16),
            pltpu.VMEM((RB + 2 * HB, 16, BS), BF16),
            pltpu.VMEM((RB + 2 * HB, 16, BS), BF16),
            pltpu.VMEM((RB + 2 * HB, 16, BS), BF16),
            pltpu.VMEM((RB + 2 * HB, 16, BS), BF16),
            pltpu.VMEM((RB, 16, BS), F32),
            pltpu.VMEM((RB, 16, BS), F32),
            pltpu.VMEM((nvec, 8, 128), BF16),
            pltpu.VMEM((nvec, 8, 128), BF16),
            pltpu.VMEM((nrow, nvec, 16, 128), BF16),
            pltpu.VMEM((64, 1024), BF16),
            pltpu.SemaphoreType.DMA((7,)),
            pltpu.SemaphoreType.DMA,
            pltpu.SemaphoreType.DMA,
            pltpu.SemaphoreType.DMA,
            pltpu.SemaphoreType.DMA,
            pltpu.SemaphoreType.DMA((4, 2)),
            pltpu.SemaphoreType.DMA((4, 2)),
            pltpu.SemaphoreType.DMA((12,)),
            pltpu.SemaphoreType.DMA((12,)),
        ],
        compiler_params=pltpu.CompilerParams(
            collective_id=0, has_side_effects=True, vmem_limit_bytes=50 << 20
        ),
    )(*[pltpu.with_memory_space_constraint(a, pltpu.HBM) for a in (vectors[0], rotation.T, blocks, column_blocks.T)])
    return out[None]


def solution(mesh):
    placed = (P("row", "vec", None), P(None, "vec"), P("row", None, None, None), P("row", None))
    return jax.shard_map(
        functools.partial(local, mesh.shape["vec"], mesh.shape["row"]),
        mesh=mesh, in_specs=placed, out_specs=P("row", "vec", None), check_vma=False,
    )
```

```python
import functools

import jax
import jax.numpy as jnp
from jax import lax
from jax.experimental import pallas as pl
from jax.experimental.pallas import tpu as pltpu
from jax.sharding import PartitionSpec as P

MESH = pl.DeviceIdType.MESH
BS = 128
HB = 2
NNZB = 8
RB = 32
Z = 16
CORES = 2
F32 = jnp.float32
BF16 = jnp.bfloat16

centre = 0.3
half_width = 1.2


def take_all(ref, sem):
    pltpu.make_async_copy(ref, ref, sem).wait()


def both_ways(q, at, size):
    return lax.rem(at + (2 * lax.rem(q, 2) - 1) * ((q + 1) // 2) + size, size)


def halves(first, second):
    low = lax.broadcasted_iota(jnp.int32, first.shape, first.ndim - 1) < 64
    axis = first.ndim - 1
    return (
        jnp.where(low, first, pltpu.roll(second, 64, axis)),
        jnp.where(low, pltpu.roll(first, 64, axis), second),
    )


def kernel(
    nvec, nrow,
    v_hbm, rt_hbm, blk_hbm, col_hbm, out_ref,
    col, v_in, rt_in, blk, send1, recv1, u0, u1, u2, u3, fa, fb, send2, recv2, rall, fbuf,
    in_sem, s1, r1, s2, r2, hs, hr, gs, gr,
):
    me = lax.axis_index("vec")
    row = lax.axis_index("row")
    core = lax.rem(row, CORES)
    yy = me // Z
    zz = lax.rem(me, Z)
    xs = nrow // CORES
    ys = nvec // Z
    first = row * RB - HB

    v_copy = pltpu.make_async_copy(v_hbm, v_in, in_sem.at[0])
    r_copy = pltpu.make_async_copy(rt_hbm, rt_in, in_sem.at[1])
    b_copies = [
        pltpu.make_async_copy(blk_hbm.at[pl.ds(8 * q, 8)], blk.at[pl.ds(8 * q, 8)], in_sem.at[2 + q])
        for q in range(4)
    ]
    c_copy = pltpu.make_async_copy(col_hbm, col, in_sem.at[6])
    v_copy.start()
    r_copy.start()
    c_copy.start()
    for c in b_copies:
        c.start()

    barrier = pltpu.get_barrier_semaphore()

    lines = [lax.rem(yy + dy, ys) * Z for dy in (2, 3, 1, 0)]

    def farthest_first(visit):
        def layer(k, _):
            z = both_ways(Z - 1 - k, zz, Z)
            for line in lines:
                visit(line + z)
            return 0

        lax.fori_loop(0, Z - 1, layer, 0)
        for line in lines[:-1]:
            visit(line + zz)

    def greet(d):
        pl.semaphore_signal(barrier, inc=1, device_id={"vec": d}, device_id_type=MESH)

    farthest_first(greet)
    for k in range(1, nrow):
        pl.semaphore_signal(barrier, inc=1, device_id={"row": lax.rem(row + k, nrow)}, device_id_type=MESH)

    v_copy.wait()
    r_copy.wait()
    for t in range(4):
        pair = jnp.concatenate(
            [v_in[:, 256 * t : 256 * t + 128], v_in[:, 256 * t + 128 : 256 * t + 256]], axis=0
        )
        turned = pair.astype(F32).T.reshape(16, 8, 128).astype(BF16)
        send1[pl.ds(16 * t, 16)] = turned
    recv1[me] = send1[me]
    rall[row, me] = rt_in[:, pl.ds(pl.multiple_of(row * 128, 128), 128)]
    zero = jnp.zeros((HB, 16, 128), BF16)
    for u in (u0, u1, u2, u3):

        @pl.when(row == 0)
        def _():
            u[pl.ds(0, HB)] = zero

        @pl.when(row == nrow - 1)
        def _():
            u[pl.ds(RB + HB, HB)] = zero

    pl.semaphore_wait(barrier, nvec - 1 + nrow - 1)

    def deal(d):
        pltpu.make_async_remote_copy(
            send1.at[d], recv1.at[me], s1, r1, device_id={"vec": d}, device_id_type=MESH
        ).start()

    farthest_first(deal)

    def along_z(k, _):
        d = yy * Z + both_ways(Z - k, zz, Z)
        pltpu.make_async_remote_copy(
            rall.at[row, me], rall.at[row, me], gs.at[0], gr.at[0],
            device_id={"vec": d}, device_id_type=MESH,
        ).start()
        return 0

    lax.fori_loop(1, Z, along_z, 0)

    def halo(step, u):
        up = pltpu.make_async_remote_copy(
            u.at[pl.ds(RB, HB)], u.at[pl.ds(0, HB)], hs.at[step, 0], hr.at[step, 0],
            device_id={"row": jnp.minimum(row + 1, nrow - 1)}, device_id_type=MESH,
        )
        down = pltpu.make_async_remote_copy(
            u.at[pl.ds(HB, HB)], u.at[pl.ds(RB + HB, HB)], hs.at[step, 1], hr.at[step, 1],
            device_id={"row": jnp.maximum(row - 1, 0)}, device_id_type=MESH,
        )
        return up, down

    def halo_start(step, u):
        up, down = halo(step, u)
        pl.when(row < nrow - 1)(up.start)
        pl.when(row > 0)(down.start)

    def halo_wait(step, u):
        up, down = halo(step, u)
        pl.when(row > 0)(up.wait_recv)
        pl.when(row < nrow - 1)(down.wait_recv)

    def halo_sent(step, u):
        up, down = halo(step, u)
        pl.when(row < nrow - 1)(up.wait_send)
        pl.when(row > 0)(down.wait_send)

    for c in b_copies:
        c.wait()

    def flip(r, _):
        for j in range(NNZB):
            blk[r, j] = blk[r, j].T
        return 0

    lax.fori_loop(0, RB, flip, 0)
    c_copy.wait()
    take_all(recv1.at[pl.ds(0, nvec - 1)], r1)
    def unpack(lo, count):
        parts = recv1[pl.ds(2 * lo, 2 * count)].astype(F32).reshape(count, 2, 8, 128)
        rows = jnp.concatenate(halves(parts[:, 0], parts[:, 1]), axis=1)
        u0[pl.ds(HB + lo, count)] = rows.astype(BF16)
        fa[pl.ds(lo, count)] = rows

    unpack(0, HB)
    unpack(RB - HB, HB)
    halo_start(0, u0)
    unpack(HB, RB - 2 * HB)

    def product(u, r):
        left = jnp.concatenate([u[jnp.clip(col[j, r] - first, 0, RB + 2 * HB - 1)] for j in range(NNZB)], axis=1)
        right = jnp.concatenate([blk[r, j] for j in range(NNZB)], axis=0)
        return jnp.dot(left, right, preferred_element_type=F32)

    def rows_of(turn, u, current, other, following, r):
        if turn == 0:
            made = (product(u, r) - centre * current[r]) / half_width
        else:
            made = 2.0 * (product(u, r) - centre * current[r]) / half_width - other[r]
        other[r] = made
        if following is not None:
            following[r + HB] = made.astype(BF16)
        return made

    def turn_of(turn, u, current, other, following):
        edge = functools.partial(rows_of, turn, u, current, other, following)
        for r in (0, 1, RB - 2, RB - 1):
            edge(r)
        halo_start(turn + 1, following)

        def inner(r, _):
            edge(r)
            return 0

        spread(turn)
        lax.fori_loop(HB, RB - HB, inner, 0, unroll=14)

    mate = row + 1 - 2 * core
    right = lax.rem(row + CORES, nrow)
    left = lax.rem(row + nrow - CORES, nrow)
    opposite = lax.rem(row + 2 * CORES, nrow)
    half = nvec // 2

    def pass_on(n, held, part, target):
        piece = rall.at[held, pl.ds(part * half, half)]
        return pltpu.make_async_remote_copy(
            piece, piece, gs.at[n], gr.at[n], device_id={"row": target}, device_id_type=MESH
        )

    def to_mate(n, held):
        return pltpu.make_async_remote_copy(
            rall.at[held], rall.at[held], gs.at[n], gr.at[n], device_id={"row": mate}, device_id_type=MESH
        )

    def spread(turn):
        if turn == 2:
            pass_on(2, row, 0, right).start()
            pass_on(3, row, 1, left).start()
        if turn == 3:
            pass_on(4, row, 1, right).start()
            pass_on(5, row, 0, left).start()
        if turn == 4:
            pass_on(2, left, 0, right).wait_recv()
            pass_on(3, right, 1, left).wait_recv()
            pass_on(6, left, 0, right).start()
            pass_on(7, right, 1, left).start()

    def along_y():
        take_all(rall.at[0, pl.ds(0, Z - 1)], gr.at[0])
        for k in range(1, ys):
            d = lax.rem(me + k * Z, nvec)
            pltpu.make_async_remote_copy(
                rall.at[row, pl.ds(yy * Z, Z)], rall.at[row, pl.ds(yy * Z, Z)], gs.at[1], gr.at[1],
                device_id={"vec": d}, device_id_type=MESH,
            ).start()

    pl.when(core == 1)(along_y)
    halo_wait(0, u0)
    turn_of(0, u0, fa, fb, u1)
    pl.when(core == 0)(along_y)
    halo_wait(1, u1)
    turn_of(1, u1, fb, fa, u2)
    take_all(rall.at[0, pl.ds(0, nvec - Z)], gr.at[1])
    to_mate(8, row).start()
    halo_wait(2, u2)
    turn_of(2, u2, fa, fb, u3)
    halo_wait(3, u3)
    spread(3)
    zpairs = Z // 2

    def finish(r):
        made = rows_of(3, u3, fb, fa, None, r)
        even, odd = halves(made[:8], made[8:])
        send2[2 * r] = even.astype(BF16)
        send2[2 * r + 1] = odd.astype(BF16)

    def give(d):
        @pl.when(d != me)
        def _():
            pltpu.make_async_remote_copy(
                send2.at[d], recv2.at[me], s2, r2, device_id={"vec": d}, device_id_type=MESH
            ).start()

    def last(g, _):
        group = [
            lax.rem(yy + dy, ys) * zpairs + (g + far)
            for dy in range(ys)
            for far in (0, zpairs // 2)
        ]
        for r in group:
            finish(r)
        for r in group:
            give(2 * r)
            give(2 * r + 1)
        return 0

    lax.fori_loop(0, zpairs // 2, last, 0)
    recv2[me] = send2[me]
    spread(4)
    pass_on(4, left, 1, right).wait_recv()
    pass_on(5, right, 0, left).wait_recv()
    to_mate(9, left).start()
    to_mate(10, right).start()
    pass_on(6, opposite, 0, right).wait_recv()
    pass_on(7, opposite, 1, left).wait_recv()
    to_mate(11, opposite).start()

    take_all(recv2.at[pl.ds(0, nvec - 1)], r2)
    for t in range(4):
        turned = recv2[pl.ds(16 * t, 16)].astype(F32).reshape(128, 128).T.astype(BF16)
        fbuf[:, 256 * t : 256 * t + 128] = turned[:64]
        fbuf[:, 256 * t + 128 : 256 * t + 256] = turned[64:]

    for n in range(8, 12):
        take_all(rall.at[0], gr.at[n])
    total = jnp.zeros((64, 1024), F32)
    for t in range(4):
        right = jnp.concatenate(
            [rall[2 * t].reshape(1024, 128), rall[2 * t + 1].reshape(1024, 128)], axis=1
        )
        total += lax.dot_general(
            fbuf[:, 256 * t : 256 * t + 256], right, (((1,), (1,)), ((), ())), preferred_element_type=F32
        )
    out_ref[...] = total.astype(BF16)

    take_all(send1.at[pl.ds(0, nvec - 1)], s1)
    take_all(send2.at[pl.ds(0, nvec - 1)], s2)
    for step, u in enumerate((u0, u1, u2, u3)):
        halo_sent(step, u)
    take_all(rall.at[0, pl.ds(0, Z - 1)], gs.at[0])
    take_all(rall.at[0, pl.ds(0, nvec - Z)], gs.at[1])
    for n in range(2, 8):
        take_all(rall.at[0, pl.ds(0, half)], gs.at[n])
    for n in range(8, 12):
        take_all(rall.at[0], gs.at[n])


def local(nvec, nrow, vectors, rotation, blocks, column_blocks):
    whole = pl.BlockSpec(memory_space=pltpu.HBM)
    out = pl.pallas_call(
        functools.partial(kernel, nvec, nrow),
        out_shape=jax.ShapeDtypeStruct((64, 1024), BF16),
        in_specs=[whole] * 4,
        out_specs=pl.BlockSpec(memory_space=pltpu.VMEM),
        scratch_shapes=[
            pltpu.SMEM((NNZB, RB), jnp.int32),
            pltpu.VMEM((64, 1024), BF16),
            pltpu.VMEM((16, 1024), BF16),
            pltpu.VMEM((RB, NNZB, BS, BS), BF16),
            pltpu.VMEM((nvec, 8, 128), BF16),
            pltpu.VMEM((nvec, 8, 128), BF16),
            pltpu.VMEM((RB + 2 * HB, 16, BS), BF16),
            pltpu.VMEM((RB + 2 * HB, 16, BS), BF16),
            pltpu.VMEM((RB + 2 * HB, 16, BS), BF16),
            pltpu.VMEM((RB + 2 * HB, 16, BS), BF16),
            pltpu.VMEM((RB, 16, BS), F32),
            pltpu.VMEM((RB, 16, BS), F32),
            pltpu.VMEM((nvec, 8, 128), BF16),
            pltpu.VMEM((nvec, 8, 128), BF16),
            pltpu.VMEM((nrow, nvec, 16, 128), BF16),
            pltpu.VMEM((64, 1024), BF16),
            pltpu.SemaphoreType.DMA((7,)),
            pltpu.SemaphoreType.DMA,
            pltpu.SemaphoreType.DMA,
            pltpu.SemaphoreType.DMA,
            pltpu.SemaphoreType.DMA,
            pltpu.SemaphoreType.DMA((4, 2)),
            pltpu.SemaphoreType.DMA((4, 2)),
            pltpu.SemaphoreType.DMA((12,)),
            pltpu.SemaphoreType.DMA((12,)),
        ],
        compiler_params=pltpu.CompilerParams(
            collective_id=0, has_side_effects=True, vmem_limit_bytes=50 << 20
        ),
    )(*[pltpu.with_memory_space_constraint(a, pltpu.HBM) for a in (vectors[0], rotation.T, blocks, column_blocks.T)])
    return out[None]


def solution(mesh):
    placed = (P("row", "vec", None), P(None, "vec"), P("row", None, None, None), P("row", None))
    return jax.shard_map(
        functools.partial(local, mesh.shape["vec"], mesh.shape["row"]),
        mesh=mesh, in_specs=placed, out_specs=P("row", "vec", None), check_vma=False,
    )
```

```python
import functools

import jax
import jax.numpy as jnp
from jax import lax
from jax.experimental import pallas as pl
from jax.experimental.pallas import tpu as pltpu
from jax.sharding import PartitionSpec as P

MESH = pl.DeviceIdType.MESH
BS = 128
HB = 2
NNZB = 8
RB = 32
Z = 16
CORES = 2
F32 = jnp.float32
BF16 = jnp.bfloat16

centre = 0.3
half_width = 1.2


def take_all(ref, sem):
    pltpu.make_async_copy(ref, ref, sem).wait()


def both_ways(q, at, size):
    return lax.rem(at + (2 * lax.rem(q, 2) - 1) * ((q + 1) // 2) + size, size)


def halves(first, second):
    low = lax.broadcasted_iota(jnp.int32, first.shape, first.ndim - 1) < 64
    axis = first.ndim - 1
    return (
        jnp.where(low, first, pltpu.roll(second, 64, axis)),
        jnp.where(low, pltpu.roll(first, 64, axis), second),
    )


def kernel(
    nvec, nrow,
    v_hbm, rt_hbm, blk_hbm, col_hbm, out_ref,
    col, v_in, rt_in, blk, send1, recv1, u0, u1, u2, u3, fa, fb, send2, recv2, rall, fbuf,
    in_sem, s1, r1, s2, r2, hs, hr, gs, gr,
):
    me = lax.axis_index("vec")
    row = lax.axis_index("row")
    core = lax.rem(row, CORES)
    yy = me // Z
    zz = lax.rem(me, Z)
    xs = nrow // CORES
    ys = nvec // Z
    first = row * RB - HB

    v_copy = pltpu.make_async_copy(v_hbm, v_in, in_sem.at[0])
    r_copy = pltpu.make_async_copy(rt_hbm, rt_in, in_sem.at[1])
    b_copies = [
        pltpu.make_async_copy(blk_hbm.at[pl.ds(8 * q, 8)], blk.at[pl.ds(8 * q, 8)], in_sem.at[2 + q])
        for q in range(4)
    ]
    c_copy = pltpu.make_async_copy(col_hbm, col, in_sem.at[6])
    v_copy.start()

    barrier = pltpu.get_barrier_semaphore()

    lines = [lax.rem(yy + dy, ys) * Z for dy in (2, 3, 1, 0)]

    def farthest_first(visit):
        def layer(k, _):
            z = both_ways(Z - 1 - k, zz, Z)
            for line in lines:
                visit(line + z)
            return 0

        lax.fori_loop(0, Z - 1, layer, 0)
        for line in lines[:-1]:
            visit(line + zz)

    def greet(d):
        pl.semaphore_signal(barrier, inc=1, device_id={"vec": d}, device_id_type=MESH)

    farthest_first(greet)
    for k in range(1, nrow):
        pl.semaphore_signal(barrier, inc=1, device_id={"row": lax.rem(row + k, nrow)}, device_id_type=MESH)

    r_copy.start()
    c_copy.start()
    for c in b_copies:
        c.start()
    v_copy.wait()
    r_copy.wait()
    for t in range(4):
        pair = jnp.concatenate(
            [v_in[:, 256 * t : 256 * t + 128], v_in[:, 256 * t + 128 : 256 * t + 256]], axis=0
        )
        turned = pair.astype(F32).T.reshape(16, 8, 128).astype(BF16)
        send1[pl.ds(16 * t, 16)] = turned
    recv1[me] = send1[me]
    rall[row, me] = rt_in[:, pl.ds(pl.multiple_of(row * 128, 128), 128)]
    zero = jnp.zeros((HB, 16, 128), BF16)
    for u in (u0, u1, u2, u3):

        @pl.when(row == 0)
        def _():
            u[pl.ds(0, HB)] = zero

        @pl.when(row == nrow - 1)
        def _():
            u[pl.ds(RB + HB, HB)] = zero

    pl.semaphore_wait(barrier, nvec - 1 + nrow - 1)

    def deal(d):
        pltpu.make_async_remote_copy(
            send1.at[d], recv1.at[me], s1, r1, device_id={"vec": d}, device_id_type=MESH
        ).start()

    farthest_first(deal)

    def along_z(k, _):
        d = yy * Z + both_ways(Z - k, zz, Z)
        pltpu.make_async_remote_copy(
            rall.at[row, me], rall.at[row, me], gs.at[0], gr.at[0],
            device_id={"vec": d}, device_id_type=MESH,
        ).start()
        return 0

    lax.fori_loop(1, Z, along_z, 0)

    def halo(step, u):
        up = pltpu.make_async_remote_copy(
            u.at[pl.ds(RB, HB)], u.at[pl.ds(0, HB)], hs.at[step, 0], hr.at[step, 0],
            device_id={"row": jnp.minimum(row + 1, nrow - 1)}, device_id_type=MESH,
        )
        down = pltpu.make_async_remote_copy(
            u.at[pl.ds(HB, HB)], u.at[pl.ds(RB + HB, HB)], hs.at[step, 1], hr.at[step, 1],
            device_id={"row": jnp.maximum(row - 1, 0)}, device_id_type=MESH,
        )
        return up, down

    def up_start(step, u):
        pl.when(row < nrow - 1)(halo(step, u)[0].start)

    def down_start(step, u):
        pl.when(row > 0)(halo(step, u)[1].start)

    def halo_start(step, u):
        up_start(step, u)
        down_start(step, u)

    def halo_wait(step, u):
        up, down = halo(step, u)
        pl.when(row > 0)(up.wait_recv)
        pl.when(row < nrow - 1)(down.wait_recv)

    def halo_sent(step, u):
        up, down = halo(step, u)
        pl.when(row < nrow - 1)(up.wait_send)
        pl.when(row > 0)(down.wait_send)

    for c in b_copies:
        c.wait()

    def flip(r, _):
        for j in range(NNZB):
            blk[r, j] = blk[r, j].T
        return 0

    lax.fori_loop(0, RB, flip, 0)
    c_copy.wait()
    take_all(recv1.at[pl.ds(0, nvec - 1)], r1)
    def unpack(lo, count):
        parts = recv1[pl.ds(2 * lo, 2 * count)].astype(F32).reshape(count, 2, 8, 128)
        rows = jnp.concatenate(halves(parts[:, 0], parts[:, 1]), axis=1)
        u0[pl.ds(HB + lo, count)] = rows.astype(BF16)
        fa[pl.ds(lo, count)] = rows

    unpack(0, HB)
    unpack(RB - HB, HB)
    halo_start(0, u0)
    unpack(HB, RB - 2 * HB)

    def product(u, r):
        left = jnp.concatenate([u[jnp.clip(col[j, r] - first, 0, RB + 2 * HB - 1)] for j in range(NNZB)], axis=1)
        right = jnp.concatenate([blk[r, j] for j in range(NNZB)], axis=0)
        return jnp.dot(left, right, preferred_element_type=F32)

    def rows_of(turn, u, current, other, following, r):
        if turn == 0:
            made = (product(u, r) - centre * current[r]) / half_width
        else:
            made = 2.0 * (product(u, r) - centre * current[r]) / half_width - other[r]
        other[r] = made
        if following is not None:
            following[r + HB] = made.astype(BF16)
        return made

    def turn_of(turn, u, current, other, following):
        edge = functools.partial(rows_of, turn, u, current, other, following)
        for r in (0, 1, RB - 2, RB - 1):
            edge(r)
        halo_start(turn + 1, following)

        def inner(r, _):
            edge(r)
            return 0

        spread(turn)
        lax.fori_loop(HB, RB - HB, inner, 0, unroll=14)

    mate = row + 1 - 2 * core
    right = lax.rem(row + CORES, nrow)
    left = lax.rem(row + nrow - CORES, nrow)
    opposite = lax.rem(row + 2 * CORES, nrow)
    half = nvec // 2

    def pass_on(n, held, part, target):
        piece = rall.at[held, pl.ds(part * half, half)]
        return pltpu.make_async_remote_copy(
            piece, piece, gs.at[n], gr.at[n], device_id={"row": target}, device_id_type=MESH
        )

    def to_mate(n, held):
        return pltpu.make_async_remote_copy(
            rall.at[held], rall.at[held], gs.at[n], gr.at[n], device_id={"row": mate}, device_id_type=MESH
        )

    def spread(turn):
        if turn == 2:
            pass_on(2, row, 0, right).start()
            pass_on(3, row, 1, left).start()
        if turn == 3:
            pass_on(4, row, 1, right).start()
            pass_on(5, row, 0, left).start()
        if turn == 4:
            pass_on(2, left, 0, right).wait_recv()
            pass_on(3, right, 1, left).wait_recv()
            pass_on(6, left, 0, right).start()
            pass_on(7, right, 1, left).start()

    def along_y():
        take_all(rall.at[0, pl.ds(0, Z - 1)], gr.at[0])
        for k in range(1, ys):
            d = lax.rem(me + k * Z, nvec)
            pltpu.make_async_remote_copy(
                rall.at[row, pl.ds(yy * Z, Z)], rall.at[row, pl.ds(yy * Z, Z)], gs.at[1], gr.at[1],
                device_id={"vec": d}, device_id_type=MESH,
            ).start()

    pl.when(core == 1)(along_y)
    halo_wait(0, u0)
    turn_of(0, u0, fa, fb, u1)
    pl.when(core == 0)(along_y)
    halo_wait(1, u1)
    turn_of(1, u1, fb, fa, u2)
    take_all(rall.at[0, pl.ds(0, nvec - Z)], gr.at[1])
    to_mate(8, row).start()
    halo_wait(2, u2)
    turn_of(2, u2, fa, fb, u3)
    halo_wait(3, u3)
    spread(3)
    zpairs = Z // 2

    def finish(r):
        made = rows_of(3, u3, fb, fa, None, r)
        even, odd = halves(made[:8], made[8:])
        send2[2 * r] = even.astype(BF16)
        send2[2 * r + 1] = odd.astype(BF16)

    def give(d):
        @pl.when(d != me)
        def _():
            pltpu.make_async_remote_copy(
                send2.at[d], recv2.at[me], s2, r2, device_id={"vec": d}, device_id_type=MESH
            ).start()

    def block_rows(rows):
        for r in rows:
            finish(r)
        for r in rows:
            give(2 * r)
            give(2 * r + 1)

    def last(g, _):
        block_rows(
            [lax.rem(yy + dy, ys) * zpairs + (g + far) for dy in range(ys) for far in (0, zpairs // 2)]
        )
        return 0

    block_rows([dy * zpairs for dy in range(ys)])
    block_rows([dy * zpairs + zpairs // 2 for dy in range(ys)])
    lax.fori_loop(1, zpairs // 2, last, 0)
    recv2[me] = send2[me]
    spread(4)
    pass_on(4, left, 1, right).wait_recv()
    pass_on(5, right, 0, left).wait_recv()
    to_mate(9, left).start()
    to_mate(10, right).start()
    pass_on(6, opposite, 0, right).wait_recv()
    pass_on(7, opposite, 1, left).wait_recv()
    to_mate(11, opposite).start()

    take_all(recv2.at[pl.ds(0, nvec - 1)], r2)
    for t in range(4):
        turned = recv2[pl.ds(16 * t, 16)].astype(F32).reshape(128, 128).T.astype(BF16)
        fbuf[:, 256 * t : 256 * t + 128] = turned[:64]
        fbuf[:, 256 * t + 128 : 256 * t + 256] = turned[64:]

    for n in range(8, 11):
        take_all(rall.at[0], gr.at[n])

    def turned_by(x):
        pair = jnp.concatenate(
            [rall[2 * x].reshape(1024, 128), rall[2 * x + 1].reshape(1024, 128)], axis=1
        )
        return lax.dot_general(
            fbuf[:, pl.ds(pl.multiple_of(256 * x, 256), 256)], pair, (((1,), (1,)), ((), ())),
            preferred_element_type=F32,
        )

    chip = row // CORES
    total = turned_by(chip) + turned_by(lax.rem(chip + 1, xs)) + turned_by(lax.rem(chip + xs - 1, xs))
    take_all(rall.at[0], gr.at[11])
    total += turned_by(lax.rem(chip + 2, xs))
    out_ref[...] = total.astype(BF16)

    take_all(send1.at[pl.ds(0, nvec - 1)], s1)
    take_all(send2.at[pl.ds(0, nvec - 1)], s2)
    for step, u in enumerate((u0, u1, u2, u3)):
        halo_sent(step, u)
    take_all(rall.at[0, pl.ds(0, Z - 1)], gs.at[0])
    take_all(rall.at[0, pl.ds(0, nvec - Z)], gs.at[1])
    for n in range(2, 8):
        take_all(rall.at[0, pl.ds(0, half)], gs.at[n])
    for n in range(8, 12):
        take_all(rall.at[0], gs.at[n])


def local(nvec, nrow, vectors, rotation, blocks, column_blocks):
    whole = pl.BlockSpec(memory_space=pltpu.HBM)
    out = pl.pallas_call(
        functools.partial(kernel, nvec, nrow),
        out_shape=jax.ShapeDtypeStruct((64, 1024), BF16),
        in_specs=[whole] * 4,
        out_specs=pl.BlockSpec(memory_space=pltpu.VMEM),
        scratch_shapes=[
            pltpu.SMEM((NNZB, RB), jnp.int32),
            pltpu.VMEM((64, 1024), BF16),
            pltpu.VMEM((16, 1024), BF16),
            pltpu.VMEM((RB, NNZB, BS, BS), BF16),
            pltpu.VMEM((nvec, 8, 128), BF16),
            pltpu.VMEM((nvec, 8, 128), BF16),
            pltpu.VMEM((RB + 2 * HB, 16, BS), BF16),
            pltpu.VMEM((RB + 2 * HB, 16, BS), BF16),
            pltpu.VMEM((RB + 2 * HB, 16, BS), BF16),
            pltpu.VMEM((RB + 2 * HB, 16, BS), BF16),
            pltpu.VMEM((RB, 16, BS), F32),
            pltpu.VMEM((RB, 16, BS), F32),
            pltpu.VMEM((nvec, 8, 128), BF16),
            pltpu.VMEM((nvec, 8, 128), BF16),
            pltpu.VMEM((nrow, nvec, 16, 128), BF16),
            pltpu.VMEM((64, 1024), BF16),
            pltpu.SemaphoreType.DMA((7,)),
            pltpu.SemaphoreType.DMA,
            pltpu.SemaphoreType.DMA,
            pltpu.SemaphoreType.DMA,
            pltpu.SemaphoreType.DMA,
            pltpu.SemaphoreType.DMA((4, 2)),
            pltpu.SemaphoreType.DMA((4, 2)),
            pltpu.SemaphoreType.DMA((12,)),
            pltpu.SemaphoreType.DMA((12,)),
        ],
        compiler_params=pltpu.CompilerParams(
            collective_id=0, has_side_effects=True, vmem_limit_bytes=50 << 20
        ),
    )(*[pltpu.with_memory_space_constraint(a, pltpu.HBM) for a in (vectors[0], rotation.T, blocks, column_blocks.T)])
    return out[None]


def solution(mesh):
    placed = (P("row", "vec", None), P(None, "vec"), P("row", None, None, None), P("row", None))
    return jax.shard_map(
        functools.partial(local, mesh.shape["vec"], mesh.shape["row"]),
        mesh=mesh, in_specs=placed, out_specs=P("row", "vec", None), check_vma=False,
    )
```

```python
import functools

import jax
import jax.numpy as jnp
from jax import lax
from jax.experimental import pallas as pl
from jax.experimental.pallas import tpu as pltpu
from jax.sharding import PartitionSpec as P

MESH = pl.DeviceIdType.MESH
BS = 128
HB = 2
NNZB = 8
RB = 32
Z = 16
CORES = 2
F32 = jnp.float32
BF16 = jnp.bfloat16

centre = 0.3
half_width = 1.2


def take_all(ref, sem):
    pltpu.make_async_copy(ref, ref, sem).wait()


def both_ways(q, at, size):
    return lax.rem(at + (2 * lax.rem(q, 2) - 1) * ((q + 1) // 2) + size, size)


def halves(first, second):
    low = lax.broadcasted_iota(jnp.int32, first.shape, first.ndim - 1) < 64
    axis = first.ndim - 1
    return (
        jnp.where(low, first, pltpu.roll(second, 64, axis)),
        jnp.where(low, pltpu.roll(first, 64, axis), second),
    )


def kernel(
    nvec, nrow,
    v_hbm, rt_hbm, blk_hbm, col_hbm, out_ref,
    col, v_in, rt_in, blk, send1, recv1, u0, u1, u2, u3, fa, fb, send2, recv2, rall, fbuf,
    in_sem, s1, r1, s2, r2, hs, hr, gs, gr,
):
    me = lax.axis_index("vec")
    row = lax.axis_index("row")
    core = lax.rem(row, CORES)
    yy = me // Z
    zz = lax.rem(me, Z)
    xs = nrow // CORES
    ys = nvec // Z
    first = row * RB - HB

    v_copy = pltpu.make_async_copy(v_hbm, v_in, in_sem.at[0])
    r_copy = pltpu.make_async_copy(rt_hbm, rt_in, in_sem.at[1])
    b_copies = [
        pltpu.make_async_copy(blk_hbm.at[pl.ds(8 * q, 8)], blk.at[pl.ds(8 * q, 8)], in_sem.at[2 + q])
        for q in range(4)
    ]
    c_copy = pltpu.make_async_copy(col_hbm, col, in_sem.at[6])
    v_copy.start()

    barrier = pltpu.get_barrier_semaphore()

    lines = [lax.rem(yy + dy, ys) * Z for dy in (2, 3, 1, 0)]

    def farthest_first(visit):
        def layer(k, _):
            z = both_ways(Z - 1 - k, zz, Z)
            for line in lines:
                visit(line + z)
            return 0

        lax.fori_loop(0, Z - 1, layer, 0)
        for line in lines[:-1]:
            visit(line + zz)

    def greet(d):
        pl.semaphore_signal(barrier, inc=1, device_id={"vec": d}, device_id_type=MESH)

    farthest_first(greet)
    for k in range(1, nrow):
        pl.semaphore_signal(barrier, inc=1, device_id={"row": lax.rem(row + k, nrow)}, device_id_type=MESH)

    r_copy.start()
    c_copy.start()
    for c in b_copies:
        c.start()
    v_copy.wait()
    r_copy.wait()
    for t in range(4):
        pair = jnp.concatenate(
            [v_in[:, 256 * t : 256 * t + 128], v_in[:, 256 * t + 128 : 256 * t + 256]], axis=0
        )
        turned = pair.astype(F32).T.reshape(16, 8, 128).astype(BF16)
        send1[pl.ds(16 * t, 16)] = turned
    recv1[me] = send1[me]
    rall[row, me] = rt_in[:, pl.ds(pl.multiple_of(row * 128, 128), 128)]
    zero = jnp.zeros((HB, 16, 128), BF16)
    for u in (u0, u1, u2, u3):

        @pl.when(row == 0)
        def _():
            u[pl.ds(0, HB)] = zero

        @pl.when(row == nrow - 1)
        def _():
            u[pl.ds(RB + HB, HB)] = zero

    pl.semaphore_wait(barrier, nvec - 1 + nrow - 1)

    def deal(d):
        pltpu.make_async_remote_copy(
            send1.at[d], recv1.at[me], s1, r1, device_id={"vec": d}, device_id_type=MESH
        ).start()

    farthest_first(deal)

    def along_z(k, _):
        d = yy * Z + both_ways(Z - k, zz, Z)
        pltpu.make_async_remote_copy(
            rall.at[row, me], rall.at[row, me], gs.at[0], gr.at[0],
            device_id={"vec": d}, device_id_type=MESH,
        ).start()
        return 0

    lax.fori_loop(1, Z, along_z, 0)

    def halo(step, u):
        up = pltpu.make_async_remote_copy(
            u.at[pl.ds(RB, HB)], u.at[pl.ds(0, HB)], hs.at[step, 0], hr.at[step, 0],
            device_id={"row": jnp.minimum(row + 1, nrow - 1)}, device_id_type=MESH,
        )
        down = pltpu.make_async_remote_copy(
            u.at[pl.ds(HB, HB)], u.at[pl.ds(RB + HB, HB)], hs.at[step, 1], hr.at[step, 1],
            device_id={"row": jnp.maximum(row - 1, 0)}, device_id_type=MESH,
        )
        return up, down

    def up_start(step, u):
        pl.when(row < nrow - 1)(halo(step, u)[0].start)

    def down_start(step, u):
        pl.when(row > 0)(halo(step, u)[1].start)

    def halo_start(step, u):
        up_start(step, u)
        down_start(step, u)

    def halo_wait(step, u):
        up, down = halo(step, u)
        pl.when(row > 0)(up.wait_recv)
        pl.when(row < nrow - 1)(down.wait_recv)

    def halo_sent(step, u):
        up, down = halo(step, u)
        pl.when(row < nrow - 1)(up.wait_send)
        pl.when(row > 0)(down.wait_send)

    for c in b_copies:
        c.wait()

    def flip(r, _):
        for j in range(NNZB):
            blk[r, j] = blk[r, j].T
        return 0

    lax.fori_loop(0, RB, flip, 0)
    c_copy.wait()
    take_all(recv1.at[pl.ds(0, nvec - 1)], r1)
    def unpack(lo, count):
        parts = recv1[pl.ds(2 * lo, 2 * count)].astype(F32).reshape(count, 2, 8, 128)
        rows = jnp.concatenate(halves(parts[:, 0], parts[:, 1]), axis=1)
        u0[pl.ds(HB + lo, count)] = rows.astype(BF16)
        fa[pl.ds(lo, count)] = rows

    unpack(0, HB)
    unpack(RB - HB, HB)
    halo_start(0, u0)
    unpack(HB, RB - 2 * HB)

    def product(u, r):
        left = jnp.concatenate([u[jnp.clip(col[j, r] - first, 0, RB + 2 * HB - 1)] for j in range(NNZB)], axis=1)
        right = jnp.concatenate([blk[r, j] for j in range(NNZB)], axis=0)
        return jnp.dot(left, right, preferred_element_type=F32)

    def rows_of(turn, u, current, other, following, r):
        if turn == 0:
            made = (product(u, r) - centre * current[r]) / half_width
        else:
            made = 2.0 * (product(u, r) - centre * current[r]) / half_width - other[r]
        other[r] = made
        if following is not None:
            following[r + HB] = made.astype(BF16)
        return made

    def turn_of(turn, u, current, other, following):
        edge = functools.partial(rows_of, turn, u, current, other, following)
        for side in (core, 1 - core):
            for r in range(HB):
                edge((RB - HB) * side + r)

            @pl.when(side == 1)
            def _():
                up_start(turn + 1, following)

            @pl.when(side == 0)
            def _():
                down_start(turn + 1, following)

        def inner(r, _):
            edge(r)
            return 0

        spread(turn)
        lax.fori_loop(HB, RB - HB, inner, 0, unroll=14)

    mate = row + 1 - 2 * core
    right = lax.rem(row + CORES, nrow)
    left = lax.rem(row + nrow - CORES, nrow)
    opposite = lax.rem(row + 2 * CORES, nrow)
    half = nvec // 2

    def pass_on(n, held, part, target):
        piece = rall.at[held, pl.ds(part * half, half)]
        return pltpu.make_async_remote_copy(
            piece, piece, gs.at[n], gr.at[n], device_id={"row": target}, device_id_type=MESH
        )

    def to_mate(n, held):
        return pltpu.make_async_remote_copy(
            rall.at[held], rall.at[held], gs.at[n], gr.at[n], device_id={"row": mate}, device_id_type=MESH
        )

    def spread(turn):
        if turn == 2:
            pass_on(2, row, 0, right).start()
            pass_on(3, row, 1, left).start()
        if turn == 3:
            pass_on(4, row, 1, right).start()
            pass_on(5, row, 0, left).start()
        if turn == 4:
            pass_on(2, left, 0, right).wait_recv()
            pass_on(3, right, 1, left).wait_recv()
            pass_on(6, left, 0, right).start()
            pass_on(7, right, 1, left).start()

    def along_y():
        take_all(rall.at[0, pl.ds(0, Z - 1)], gr.at[0])
        for k in range(1, ys):
            d = lax.rem(me + k * Z, nvec)
            pltpu.make_async_remote_copy(
                rall.at[row, pl.ds(yy * Z, Z)], rall.at[row, pl.ds(yy * Z, Z)], gs.at[1], gr.at[1],
                device_id={"vec": d}, device_id_type=MESH,
            ).start()

    pl.when(core == 1)(along_y)
    halo_wait(0, u0)
    turn_of(0, u0, fa, fb, u1)
    pl.when(core == 0)(along_y)
    halo_wait(1, u1)
    turn_of(1, u1, fb, fa, u2)
    take_all(rall.at[0, pl.ds(0, nvec - Z)], gr.at[1])
    to_mate(8, row).start()
    halo_wait(2, u2)
    turn_of(2, u2, fa, fb, u3)
    halo_wait(3, u3)
    spread(3)
    zpairs = Z // 2

    def finish(r):
        made = rows_of(3, u3, fb, fa, None, r)
        even, odd = halves(made[:8], made[8:])
        send2[2 * r] = even.astype(BF16)
        send2[2 * r + 1] = odd.astype(BF16)

    def give(d):
        @pl.when(d != me)
        def _():
            pltpu.make_async_remote_copy(
                send2.at[d], recv2.at[me], s2, r2, device_id={"vec": d}, device_id_type=MESH
            ).start()

    def block_rows(rows):
        for r in rows:
            finish(r)
        for r in rows:
            give(2 * r)
            give(2 * r + 1)

    def last(g, _):
        block_rows(
            [lax.rem(yy + dy, ys) * zpairs + (g + far) for dy in range(ys) for far in (0, zpairs // 2)]
        )
        return 0

    block_rows([dy * zpairs for dy in range(ys)])
    block_rows([dy * zpairs + zpairs // 2 for dy in range(ys)])
    lax.fori_loop(1, zpairs // 2, last, 0)
    recv2[me] = send2[me]
    spread(4)
    pass_on(4, left, 1, right).wait_recv()
    pass_on(5, right, 0, left).wait_recv()
    to_mate(9, left).start()
    to_mate(10, right).start()
    pass_on(6, opposite, 0, right).wait_recv()
    pass_on(7, opposite, 1, left).wait_recv()
    to_mate(11, opposite).start()

    take_all(recv2.at[pl.ds(0, nvec - 1)], r2)
    for t in range(4):
        turned = recv2[pl.ds(16 * t, 16)].astype(F32).reshape(128, 128).T.astype(BF16)
        fbuf[:, 256 * t : 256 * t + 128] = turned[:64]
        fbuf[:, 256 * t + 128 : 256 * t + 256] = turned[64:]

    for n in range(8, 11):
        take_all(rall.at[0], gr.at[n])

    def turned_by(x):
        pair = jnp.concatenate(
            [rall[2 * x].reshape(1024, 128), rall[2 * x + 1].reshape(1024, 128)], axis=1
        )
        return lax.dot_general(
            fbuf[:, pl.ds(pl.multiple_of(256 * x, 256), 256)], pair, (((1,), (1,)), ((), ())),
            preferred_element_type=F32,
        )

    chip = row // CORES
    total = turned_by(chip) + turned_by(lax.rem(chip + 1, xs)) + turned_by(lax.rem(chip + xs - 1, xs))
    take_all(rall.at[0], gr.at[11])
    total += turned_by(lax.rem(chip + 2, xs))
    out_ref[...] = total.astype(BF16)

    take_all(send1.at[pl.ds(0, nvec - 1)], s1)
    take_all(send2.at[pl.ds(0, nvec - 1)], s2)
    for step, u in enumerate((u0, u1, u2, u3)):
        halo_sent(step, u)
    take_all(rall.at[0, pl.ds(0, Z - 1)], gs.at[0])
    take_all(rall.at[0, pl.ds(0, nvec - Z)], gs.at[1])
    for n in range(2, 8):
        take_all(rall.at[0, pl.ds(0, half)], gs.at[n])
    for n in range(8, 12):
        take_all(rall.at[0], gs.at[n])


def local(nvec, nrow, vectors, rotation, blocks, column_blocks):
    whole = pl.BlockSpec(memory_space=pltpu.HBM)
    out = pl.pallas_call(
        functools.partial(kernel, nvec, nrow),
        out_shape=jax.ShapeDtypeStruct((64, 1024), BF16),
        in_specs=[whole] * 4,
        out_specs=pl.BlockSpec(memory_space=pltpu.VMEM),
        scratch_shapes=[
            pltpu.SMEM((NNZB, RB), jnp.int32),
            pltpu.VMEM((64, 1024), BF16),
            pltpu.VMEM((16, 1024), BF16),
            pltpu.VMEM((RB, NNZB, BS, BS), BF16),
            pltpu.VMEM((nvec, 8, 128), BF16),
            pltpu.VMEM((nvec, 8, 128), BF16),
            pltpu.VMEM((RB + 2 * HB, 16, BS), BF16),
            pltpu.VMEM((RB + 2 * HB, 16, BS), BF16),
            pltpu.VMEM((RB + 2 * HB, 16, BS), BF16),
            pltpu.VMEM((RB + 2 * HB, 16, BS), BF16),
            pltpu.VMEM((RB, 16, BS), F32),
            pltpu.VMEM((RB, 16, BS), F32),
            pltpu.VMEM((nvec, 8, 128), BF16),
            pltpu.VMEM((nvec, 8, 128), BF16),
            pltpu.VMEM((nrow, nvec, 16, 128), BF16),
            pltpu.VMEM((64, 1024), BF16),
            pltpu.SemaphoreType.DMA((7,)),
            pltpu.SemaphoreType.DMA,
            pltpu.SemaphoreType.DMA,
            pltpu.SemaphoreType.DMA,
            pltpu.SemaphoreType.DMA,
            pltpu.SemaphoreType.DMA((4, 2)),
            pltpu.SemaphoreType.DMA((4, 2)),
            pltpu.SemaphoreType.DMA((12,)),
            pltpu.SemaphoreType.DMA((12,)),
        ],
        compiler_params=pltpu.CompilerParams(
            collective_id=0, has_side_effects=True, vmem_limit_bytes=50 << 20
        ),
    )(*[pltpu.with_memory_space_constraint(a, pltpu.HBM) for a in (vectors[0], rotation.T, blocks, column_blocks.T)])
    return out[None]


def solution(mesh):
    placed = (P("row", "vec", None), P(None, "vec"), P("row", None, None, None), P("row", None))
    return jax.shard_map(
        functools.partial(local, mesh.shape["vec"], mesh.shape["row"]),
        mesh=mesh, in_specs=placed, out_specs=P("row", "vec", None), check_vma=False,
    )
```
